32 devices in a mesh: wide: 16 (over z, y, core), narrow: 2 (over x).
Axes of the slice: x: 2, y: 2, z: 4, core: 2. Of those that a mesh axis runs over, the one named last changes fastest.
Arguments:
- residual: bfloat16 [384, 5120], P(None, 'narrow'), may hold values from -70 to 70
- norm_gain: bfloat16 [5120], P('narrow'), may hold values from 0.5 to 1.5
- grad_out: bfloat16 [384, 5120], P(None, 'narrow'), may hold values from -6 to 6
- w_gate: bfloat16 [5120, 27648], P('narrow', 'wide'), may hold values from -0.078125 to 0.078125
- w_up: bfloat16 [5120, 27648], P('narrow', 'wide'), may hold values from -0.078125 to 0.078125
- w_down: bfloat16 [27648, 5120], P('wide', 'narrow'), may hold values from -0.0390625 to 0.0390625
- w_output: bfloat16 [5120, 5120], P('narrow', 'wide'), may hold values from -0.078125 to 0.078125
- query: bfloat16 [384, 5120], P('narrow'), may hold values from -6 to 6
- key: bfloat16 [384, 1024], P('narrow'), may hold values from -6 to 6
- value: bfloat16 [384, 1024], P('narrow'), may hold values from -6 to 6
- cache_key: bfloat16 [32768, 1024], P('wide', 'narrow'), may hold values from -10 to 10
- cache_value: bfloat16 [32768, 1024], P('wide', 'narrow'), may hold values from -6 to 6
- visible_from: int32 [384], replicated, may hold values from 0 to 16383
Outputs:
- grad_residual: bfloat16 [384, 5120], P(None, 'narrow')
- grad_gain: float32 [5120], P('narrow')
- grad_w_gate: bfloat16 [5120, 27648], P('narrow', 'wide')
- grad_w_up: bfloat16 [5120, 27648], P('narrow', 'wide')
- grad_w_down: bfloat16 [27648, 5120], P('wide', 'narrow')
- grad_w_output: bfloat16 [5120, 5120], P('narrow', 'wide')
- grad_query: bfloat16 [384, 5120], P(None, 'narrow')
The draws below stay inside these ranges and needn't reach their ends.
All inputs are finite; a program needn't handle non-finite values.
Results may differ from the reference program's by a relative error of at most 0.01.
Values may be sent and summed in bfloat16 or wider, within the bound.
A program may use at most 320 MiB of HBM per device.

```python
import math
import jax
import jax.numpy as jnp
from jax import lax

D = 5120
FF = 27648
HEADS = 40
KV_HEADS = 8
HEAD_DIM = 128
TOKENS = 384
CONTEXT = 32768


def draw_residual(key, part):
    first, second, third = jax.random.split(key, 3)
    rows = jnp.exp(jax.random.uniform(first, (TOKENS, 1), jnp.float32, math.log(0.3), math.log(3.0)))
    ramp = jnp.arange(D, dtype=jnp.float32) / D
    jitter = jnp.exp(jax.random.uniform(second, (1, D), jnp.float32, -0.3, 0.3))
    columns = (10.0 ** (ramp - 0.5))[None, :] * jitter
    base = jnp.clip(jax.random.normal(third, (TOKENS, D), jnp.float32), -5.0, 5.0)
    return (base * rows * columns).astype(jnp.bfloat16)


def attention_pair(key):
    base_seed = jax.random.fold_in(key, 11)
    query_seed, key_seed = jax.random.split(base_seed, 2)
    group = HEADS // KV_HEADS
    queries = jnp.clip(jax.random.normal(query_seed, (TOKENS, KV_HEADS, group, HEAD_DIM), jnp.float32), -5.0, 5.0)
    keys = jnp.clip(jax.random.normal(key_seed, (TOKENS, KV_HEADS, HEAD_DIM), jnp.float32), -5.0, 5.0)
    return (queries.reshape(TOKENS, HEADS * HEAD_DIM), keys.reshape(TOKENS, KV_HEADS * HEAD_DIM))


def draw_query(key, part):
    return attention_pair(key)[0].astype(jnp.bfloat16)


def draw_key(key, part):
    return attention_pair(key)[1].astype(jnp.bfloat16)


def draw_cache_key(key, part):
    ramp = jnp.arange(CONTEXT, dtype=jnp.float32) / CONTEXT
    factor = 10.0 ** (0.5 * ramp - 0.25)
    base = jnp.clip(jax.random.normal(key, (CONTEXT, KV_HEADS * HEAD_DIM), jnp.float32), -5.0, 5.0)
    return (base * factor[:, None]).astype(jnp.bfloat16)


def with_ends(result, rng, smallest, largest):
    longest = result.shape.index(max(result.shape))
    spots = []
    for shift in (0, 1):
        where = [jax.random.randint(jax.random.fold_in(rng, axis), (), 0, length) for axis, length in enumerate(result.shape)]
        where[longest] = (where[longest] + shift) % result.shape[longest]
        spots.append(tuple(where))
    return result.at[spots[0]].set(smallest).at[spots[1]].set(largest)


def block_levels(own_key, extent, cuts, least, largest):
    loudness = 1.0
    for axis_at, parts in cuts:
        heights = jax.random.uniform(jax.random.fold_in(jax.random.fold_in(own_key, 6), axis_at), (parts,), jnp.float32, least / len(cuts), largest / len(cuts))
        loudness = loudness * jnp.repeat(jnp.exp(heights), extent[axis_at] // parts).reshape((-1,) + (1,) * (len(extent) - 1 - axis_at))
    return loudness


def gaussian(key, shape, width, limit, pieces=(), kind=jnp.bfloat16):
    loudness = block_levels(key, shape, pieces, -0.22, 0.18) if pieces else 1.0
    result = jax.random.normal(key, shape, jnp.float32) * width * loudness
    return jnp.minimum(jnp.maximum(result, -limit), limit).astype(kind)


def setup_inputs(seed: int = 0) -> dict:
    arg_keys = jax.random.split(jax.random.key(seed), 14)
    return {
        "residual": draw_residual(jax.random.fold_in(arg_keys[13], 71), 0),
        "norm_gain": jnp.clip(1.0 + 0.1 * jax.random.normal(arg_keys[1], (D,), jnp.float32), 0.5, 1.5).astype(jnp.bfloat16),
        "grad_out": gaussian(arg_keys[2], (TOKENS, D), 1.0, 6.0, ((1, 2),)),
        "w_gate": gaussian(arg_keys[3], (D, FF), D ** -0.5, 0.078125, ((0, 2), (1, 16))),
        "w_up": gaussian(arg_keys[4], (D, FF), D ** -0.5, 0.078125, ((0, 2), (1, 16))),
        "w_down": gaussian(arg_keys[5], (FF, D), FF ** -0.5, 0.0390625, ((0, 16), (1, 2))),
        "w_output": gaussian(arg_keys[6], (HEADS * HEAD_DIM, D), (HEADS * HEAD_DIM) ** -0.5, 0.078125, ((0, 2), (1, 16))),
        "query": draw_query(jax.random.fold_in(arg_keys[13], 71), 0),
        "key": draw_key(jax.random.fold_in(arg_keys[13], 71), 0),
        "value": gaussian(arg_keys[9], (TOKENS, KV_HEADS * HEAD_DIM), 1.0, 6.0, ((0, 2),)),
        "cache_key": draw_cache_key(jax.random.fold_in(arg_keys[13], 71), 0),
        "cache_value": gaussian(arg_keys[11], (CONTEXT, KV_HEADS * HEAD_DIM), 1.0, 6.0, ((0, 16), (1, 2))),
        "visible_from": with_ends(jax.random.randint(arg_keys[12], (TOKENS,), 0, CONTEXT // 2), jax.random.fold_in(arg_keys[12], 1), 0, (CONTEXT // 2) - 1).astype(jnp.int32),
    }


EPSILON = 1e-06

def reference(residual, norm_gain, grad_out, w_gate, w_up, w_down, w_output, query, key, value, cache_key, cache_value, visible_from):
    stream = residual.astype(jnp.float32)
    gain = norm_gain.astype(jnp.float32)
    rstd = lax.rsqrt(lax.optimization_barrier(jnp.mean(stream * stream, axis=1, keepdims=True)) + EPSILON)
    scaled = stream * rstd
    normed = (scaled * gain).astype(jnp.bfloat16)
    gate = jnp.dot(normed, w_gate, preferred_element_type=jnp.float32)
    up = jnp.dot(normed, w_up, preferred_element_type=jnp.float32)
    hidden_grad = jnp.dot(grad_out, w_down.T, preferred_element_type=jnp.float32)
    sigmoid_gate = jax.nn.sigmoid(gate)
    silu_gate = gate * sigmoid_gate
    activated = (silu_gate * up).astype(jnp.bfloat16)
    d_gate = (hidden_grad * up * sigmoid_gate * (1.0 + gate * (1.0 - sigmoid_gate))).astype(jnp.bfloat16)
    d_up = (hidden_grad * silu_gate).astype(jnp.bfloat16)
    grad_w_down = jnp.dot(activated.T, grad_out, preferred_element_type=jnp.float32).astype(jnp.bfloat16)
    grad_w_gate = jnp.dot(normed.T, d_gate, preferred_element_type=jnp.float32).astype(jnp.bfloat16)
    grad_w_up = jnp.dot(normed.T, d_up, preferred_element_type=jnp.float32).astype(jnp.bfloat16)
    d_normed = jnp.dot(d_gate, w_gate.T, preferred_element_type=jnp.float32) + jnp.dot(d_up, w_up.T, preferred_element_type=jnp.float32)
    grad_gain = lax.optimization_barrier(jnp.sum(d_normed * scaled, axis=0))
    weighted = d_normed * gain
    inner = lax.optimization_barrier(jnp.mean(weighted * scaled, axis=1, keepdims=True))
    grad_residual = (grad_out.astype(jnp.float32) + rstd * (weighted - scaled * inner)).astype(jnp.bfloat16)
    d_attention = jnp.dot(grad_residual, w_output.T, preferred_element_type=jnp.float32).astype(jnp.bfloat16)
    group = HEADS // KV_HEADS
    every_key = jnp.concatenate([cache_key, key], axis=0).reshape(CONTEXT + TOKENS, KV_HEADS, HEAD_DIM).transpose(1, 0, 2)
    every_value = jnp.concatenate([cache_value, value], axis=0).reshape(CONTEXT + TOKENS, KV_HEADS, HEAD_DIM).transpose(1, 0, 2)
    queries = query.reshape(TOKENS, HEADS, HEAD_DIM).transpose(1, 0, 2)
    incoming = d_attention.reshape(TOKENS, HEADS, HEAD_DIM).transpose(1, 0, 2)
    position = jnp.arange(TOKENS, dtype=jnp.int32)[:, None]
    slots = jnp.arange(CONTEXT + TOKENS, dtype=jnp.int32)[None, :]
    usable = jnp.where(slots < CONTEXT, slots >= visible_from[:, None], slots - CONTEXT <= position)
    scale = 1.0 / math.sqrt(HEAD_DIM)

    def one_head(inputs):
        head_query, head_grad, index = inputs
        head_keys = lax.dynamic_index_in_dim(every_key, (index // group).astype(jnp.int32), 0, keepdims=False)
        head_values = lax.dynamic_index_in_dim(every_value, (index // group).astype(jnp.int32), 0, keepdims=False)
        scores = jnp.dot(head_query, head_keys.T, preferred_element_type=jnp.float32) * scale
        scores = jnp.where(usable, scores, -1e+30)
        highest = lax.optimization_barrier(jnp.max(scores, axis=1, keepdims=True))
        weights = jnp.where(usable, jnp.exp(scores - highest), 0.0)
        probs = weights / lax.optimization_barrier(jnp.sum(weights, axis=1, keepdims=True))
        probs_low = probs.astype(jnp.bfloat16)
        attended = jnp.dot(probs_low, head_values, preferred_element_type=jnp.float32).astype(jnp.bfloat16)
        prob_grad = jnp.dot(head_grad, head_values.T, preferred_element_type=jnp.float32)
        delta = lax.optimization_barrier(jnp.sum(head_grad.astype(jnp.float32) * attended.astype(jnp.float32), axis=1, keepdims=True))
        score_grad = (probs * (prob_grad - delta)).astype(jnp.bfloat16)
        head_query_grad = (jnp.dot(score_grad, head_keys, preferred_element_type=jnp.float32) * scale).astype(jnp.bfloat16)
        return (attended, head_query_grad)
    attended, query_grads = lax.map(one_head, (queries, incoming, jnp.arange(HEADS, dtype=jnp.int32)))
    attended = attended.transpose(1, 0, 2).reshape(TOKENS, HEADS * HEAD_DIM)
    grad_query = query_grads.transpose(1, 0, 2).reshape(TOKENS, HEADS * HEAD_DIM)
    grad_w_output = jnp.dot(attended.T, grad_residual, preferred_element_type=jnp.float32).astype(jnp.bfloat16)
    return (grad_residual, grad_gain, grad_w_gate, grad_w_up, grad_w_down, grad_w_output, grad_query)
```

```python
import functools
import math

import jax
import jax.numpy as jnp
from jax import lax
from jax.experimental import pallas as pl
from jax.experimental.pallas import tpu as pltpu
from jax.sharding import PartitionSpec as P

D = 5120
HEAD_DIM = 128


EPSILON = 1e-06


def contract_rows(left, right):
    return lax.dot_general(
        left, right, (((0,), (0,)), ((), ())), preferred_element_type=jnp.float32
    )


def contract_cols(left, right):
    return lax.dot_general(
        left, right, (((1,), (1,)), ((), ())), preferred_element_type=jnp.float32
    )


def swapped(array, axis, bit):
    size = lax.axis_size(axis)
    return lax.ppermute(array, axis, [(i, i ^ (1 << bit)) for i in range(size)])


def wide_bits():
    return lax.axis_size("wide").bit_length() - 1


def bit_of(k):
    return (lax.axis_index("wide") >> k) & 1


def as_cube(array):
    count = lax.axis_size("wide")
    return array.reshape((2,) * wide_bits() + (array.shape[0] // count, array.shape[1]))


def scatter_sum(cube, order):
    for k in order:
        bit = bit_of(k)
        sent = lax.dynamic_slice_in_dim(cube, 1 - bit, 1, k).astype(jnp.bfloat16)
        kept = lax.dynamic_slice_in_dim(cube, bit, 1, k).astype(jnp.float32)
        cube = kept + swapped(sent, "wide", k).astype(jnp.float32)
    return cube.reshape(cube.shape[-2:])


def gathered(chunk, order):
    cube = chunk.reshape((1,) * wide_bits() + chunk.shape)
    for k in reversed(order):
        other = swapped(cube, "wide", k)
        first = bit_of(k) == 0
        cube = jnp.concatenate(
            [jnp.where(first, cube, other), jnp.where(first, other, cube)], axis=k
        )
    return cube.reshape(-1, cube.shape[-1])


def own_rows(array):
    bits = wide_bits()
    rows = array.shape[0] // lax.axis_size("wide")
    at = sum(bit_of(k) << (bits - 1 - k) for k in range(bits))
    return lax.dynamic_slice_in_dim(array, at * rows, rows, 0)


def doubled(value, combine):
    for k in range(wide_bits()):
        value = combine(value, swapped(value, "wide", k))
    return value


def orders():
    bits = wide_bits()
    plain = list(range(bits))
    return (plain, plain[:1] + plain[2:] + plain[1:2])


def narrow_sum(part):
    if lax.axis_size("narrow") == 2:
        return part + swapped(part, "narrow", 0)
    return lax.psum(part, "narrow")


def narrow_total(part):
    if lax.axis_size("narrow") == 2:
        return part + swapped(part.astype(jnp.bfloat16), "narrow", 0).astype(jnp.float32)
    return lax.psum(part, "narrow")


def to_heads(rows):
    if lax.axis_size("narrow") != 2:
        return lax.all_to_all(rows, "narrow", split_axis=1, concat_axis=0, tiled=True)
    place = lax.axis_index("narrow")
    half = rows.shape[1] // 2
    count = rows.shape[0] // 2
    bit = bit_of(0)
    kept = lax.dynamic_slice_in_dim(rows, place * half, half, 1)
    sent = lax.dynamic_slice(rows, (bit * count, (1 - place) * half), (count, half))
    got = swapped(sent, "narrow", 0)
    other = swapped(got, "wide", 0)
    first = bit == 0
    far = jnp.concatenate([jnp.where(first, got, other), jnp.where(first, other, got)], axis=0)
    low = place == 0
    return jnp.concatenate([jnp.where(low, kept, far), jnp.where(low, far, kept)], axis=0)


def merge_softmax(base, first, second):
    heads = first.shape[1] // 2
    top = jnp.maximum(first[:, :heads], second[:, :heads])
    total = first[:, heads:] * jnp.exp2((first[:, :heads] - top) * base) + second[
        :, heads:
    ] * jnp.exp2((second[:, :heads] - top) * base)
    return jnp.concatenate([top, total], axis=1)


def swiglu_back(gate, up, hidden_grad):
    sigmoid_gate = jax.nn.sigmoid(gate)
    silu_gate = gate * sigmoid_gate
    activated = (silu_gate * up).astype(jnp.bfloat16)
    d_gate = (hidden_grad * up * sigmoid_gate * (1.0 + gate * (1.0 - sigmoid_gate))).astype(
        jnp.bfloat16
    )
    d_up = (hidden_grad * silu_gate).astype(jnp.bfloat16)
    return (activated, d_gate, d_up)


LOG2E = 1.4426950408889634
MASKED = -1e30


def raw_scores(q, key_ref, own_key_ref, from_ref, own_ref):
    cached = contract_cols(q, key_ref[...])
    at = lax.broadcasted_iota(jnp.int32, cached.shape, 1)
    cached = jnp.where(at >= from_ref[...], cached, MASKED)
    own = contract_cols(q, own_key_ref[...])
    own_at = lax.broadcasted_iota(jnp.int32, own.shape, 1)
    own = jnp.where(own_at <= own_ref[...], own, MASKED)
    return (cached, own)


def pick_lane(stat_ref, head):
    lane = lax.broadcasted_iota(jnp.int32, stat_ref.shape, 1)
    return jnp.sum(jnp.where(lane == head, stat_ref[...], 0.0), axis=1, keepdims=True)


def forward_kernel(
    base, q_ref, key_ref, value_ref, own_key_ref, own_value_ref,
    from_ref, own_ref, out_ref, top_ref, total_ref,
):
    head = pl.program_id(0)

    @pl.when(head == 0)
    def _():
        top_ref[...] = jnp.zeros_like(top_ref)
        total_ref[...] = jnp.zeros_like(total_ref)

    cached, own = raw_scores(q_ref[...], key_ref, own_key_ref, from_ref, own_ref)
    top = jnp.maximum(
        jnp.max(cached, axis=1, keepdims=True), jnp.max(own, axis=1, keepdims=True)
    )
    cached = jnp.exp2((cached - top) * base)
    own = jnp.exp2((own - top) * base)
    total = jnp.sum(cached, axis=1, keepdims=True) + jnp.sum(own, axis=1, keepdims=True)
    out = jnp.dot(
        cached.astype(jnp.bfloat16), value_ref[...], preferred_element_type=jnp.float32
    ) + jnp.dot(
        own.astype(jnp.bfloat16), own_value_ref[...], preferred_element_type=jnp.float32
    )
    out_ref[...] = out.astype(out_ref.dtype)
    lane = lax.broadcasted_iota(jnp.int32, top_ref.shape, 1)
    top_ref[...] = jnp.where(lane == head, top, top_ref[...])
    total_ref[...] = jnp.where(lane == head, total, total_ref[...])


def backward_kernel(
    first_head, base, scale, q_ref, grad_ref, attended_ref, key_ref, value_ref,
    own_key_ref, own_value_ref, from_ref, own_ref, top_ref, inverse_ref, out_ref,
):
    head = first_head + pl.program_id(0)
    cached, own = raw_scores(q_ref[...], key_ref, own_key_ref, from_ref, own_ref)
    top = pick_lane(top_ref, head)
    inverse = pick_lane(inverse_ref, head)
    grad = grad_ref[...]
    delta = jnp.sum(
        grad.astype(jnp.float32) * attended_ref[...].astype(jnp.float32),
        axis=1,
        keepdims=True,
    )
    cached = jnp.exp2((cached - top) * base) * (contract_cols(grad, value_ref[...]) - delta)
    own = jnp.exp2((own - top) * base) * (contract_cols(grad, own_value_ref[...]) - delta)
    out = jnp.dot(
        cached.astype(jnp.bfloat16), key_ref[...], preferred_element_type=jnp.float32
    ) + jnp.dot(
        own.astype(jnp.bfloat16), own_key_ref[...], preferred_element_type=jnp.float32
    )
    out_ref[...] = (out * (inverse * scale)).astype(out_ref.dtype)


def blocks(tokens, cached, padded, group, first):
    head = pl.BlockSpec((tokens, HEAD_DIM), lambda p: (0, first + p))
    rows = pl.BlockSpec((cached, HEAD_DIM), lambda p: (0, group))
    own = pl.BlockSpec((padded, HEAD_DIM), lambda p: (0, group))
    bound = pl.BlockSpec((tokens, 1), lambda p: (0, 0))
    stat = pl.BlockSpec((tokens, HEAD_DIM), lambda p: (0, 0))
    return (head, rows, own, bound, stat)


def forward_group(group, per_group, base, queries, keys, values, own_keys, own_values, bounds):
    tokens = queries.shape[0]
    cached, padded = keys.shape[0], own_keys.shape[0]
    head, rows, own, bound, stat = blocks(tokens, cached, padded, group, group * per_group)
    out = pl.BlockSpec((tokens, HEAD_DIM), lambda p: (0, p))
    work = per_group * tokens * (cached + padded)
    return pl.pallas_call(
        functools.partial(forward_kernel, base),
        grid=(per_group,),
        in_specs=[head, rows, rows, own, own, bound, bound],
        out_specs=[out, stat, stat],
        out_shape=[
            jax.ShapeDtypeStruct((tokens, per_group * HEAD_DIM), jnp.float32),
            jax.ShapeDtypeStruct((tokens, HEAD_DIM), jnp.float32),
            jax.ShapeDtypeStruct((tokens, HEAD_DIM), jnp.float32),
        ],
        compiler_params=pltpu.CompilerParams(vmem_limit_bytes=40 << 20),
        cost_estimate=pl.CostEstimate(
            flops=4 * HEAD_DIM * work, bytes_accessed=6 << 20, transcendentals=work
        ),
    )(queries, keys, values, own_keys, own_values, *bounds)


def backward_group(
    group, per_group, base, scale, queries, grads, attended, keys, values,
    own_keys, own_values, bounds, top, inverse, shift,
):
    tokens = queries.shape[0]
    cached, padded = keys.shape[0], own_keys.shape[0]
    first = group * per_group
    head, rows, own, bound, stat = blocks(tokens, cached, padded, group, first)
    grad = pl.BlockSpec((tokens, HEAD_DIM), lambda p: (0, first - shift + p))
    out = pl.BlockSpec((tokens, HEAD_DIM), lambda p: (0, p))
    work = per_group * tokens * (cached + padded)
    return pl.pallas_call(
        functools.partial(backward_kernel, first, base, scale),
        grid=(per_group,),
        in_specs=[head, grad, head, rows, rows, own, own, bound, bound, stat, stat],
        out_specs=out,
        out_shape=jax.ShapeDtypeStruct((tokens, per_group * HEAD_DIM), jnp.float32),
        compiler_params=pltpu.CompilerParams(vmem_limit_bytes=48 << 20),
        cost_estimate=pl.CostEstimate(
            flops=6 * HEAD_DIM * work, bytes_accessed=6 << 20, transcendentals=work
        ),
    )(queries, grads, attended, keys, values, own_keys, own_values, *bounds, top, inverse)


def split_columns(array, pieces):
    width = array.shape[1] // pieces
    return [array[:, i * width : (i + 1) * width] for i in range(pieces)]


def per_device(
    residual,
    norm_gain,
    grad_out,
    w_gate,
    w_up,
    w_down,
    w_output,
    query,
    key,
    value,
    cache_key,
    cache_value,
    visible_from,
):
    wide_count = lax.axis_size("wide")
    wide_place = lax.axis_index("wide")
    tokens = residual.shape[0]
    scale = 1.0 / math.sqrt(HEAD_DIM)
    base = scale * LOG2E

    stream = residual.astype(jnp.float32)
    gain = norm_gain.astype(jnp.float32)
    hidden_part = contract_cols(grad_out, w_down)
    squares = narrow_sum(jnp.sum(stream * stream, axis=1))
    rstd = lax.rsqrt(squares / D + EPSILON)[:, None]
    normed = (stream * rstd * gain).astype(jnp.bfloat16)
    gate_part = jnp.dot(normed, w_gate, preferred_element_type=jnp.float32)
    up_part = jnp.dot(normed, w_up, preferred_element_type=jnp.float32)

    queries, stretch_keys, stretch_values = (to_heads(query), to_heads(key), to_heads(value))
    groups = stretch_keys.shape[1] // HEAD_DIM
    per_group = queries.shape[1] // stretch_keys.shape[1]
    heads = groups * per_group
    cached = cache_key.shape[0]
    span = tokens // wide_count
    start = wide_place * span
    padded = -(-span // HEAD_DIM) * HEAD_DIM
    filler = ((0, padded - span), (0, 0))
    own_keys = jnp.pad(lax.dynamic_slice_in_dim(stretch_keys, start, span, 0), filler)
    own_values = jnp.pad(lax.dynamic_slice_in_dim(stretch_values, start, span, 0), filler)
    position = jnp.arange(tokens, dtype=jnp.int32)[:, None]
    bounds = (
        visible_from[:, None] - wide_place * cached,
        jnp.minimum(position - start, span - 1),
    )

    hidden_grad = narrow_total(hidden_part)
    gate = narrow_total(gate_part)
    up = narrow_total(up_part)

    outs, tops, totals = [], [], []
    for group in range(groups):
        out, top, total = forward_group(
            group, per_group, base, queries, cache_key, cache_value, own_keys, own_values, bounds
        )
        outs.append(out)
        tops.append(top[:, :per_group])
        totals.append(total[:, :per_group])
    local_top = jnp.concatenate(tops, axis=1)
    stats = doubled(
        jnp.concatenate([local_top] + totals, axis=1), functools.partial(merge_softmax, base)
    )
    top, inverse = stats[:, :heads], 1.0 / stats[:, heads:]
    factor = jnp.exp2((local_top - top) * base) * inverse
    spread = jnp.repeat(factor, HEAD_DIM, axis=1)
    attended_part = jnp.concatenate(outs, axis=1) * spread
    side = ((0, 0), (0, HEAD_DIM - heads))
    top, inverse = jnp.pad(top, side), jnp.pad(inverse, side)
    ways = orders()
    attended = jnp.concatenate(
        [
            gathered(scatter_sum(as_cube(part), way).astype(jnp.bfloat16), way)
            for part, way in zip(split_columns(attended_part, 2), ways)
        ],
        axis=1,
    )

    activated, d_gate, d_up = swiglu_back(gate, up, hidden_grad)
    d_normed_part = contract_cols(d_gate, w_gate) + contract_cols(d_up, w_up)
    grad_w_down = contract_rows(activated, grad_out).astype(jnp.bfloat16)
    grad_w_gate = contract_rows(normed, d_gate).astype(jnp.bfloat16)
    grad_w_up = contract_rows(normed, d_up).astype(jnp.bfloat16)
    d_normed = jnp.concatenate(
        [
            scatter_sum(as_cube(part), way)
            for part, way in zip(split_columns(d_normed_part, 2), ways)
        ],
        axis=1,
    )
    rstd_rows = own_rows(rstd)
    scaled = own_rows(residual).astype(jnp.float32) * rstd_rows
    grad_gain = doubled(jnp.sum(d_normed * scaled, axis=0), jnp.add)
    weighted = d_normed * gain
    inner = narrow_sum(jnp.sum(weighted * scaled, axis=1)) / D
    grad_rows = (
        own_rows(grad_out).astype(jnp.float32)
        + rstd_rows * (weighted - scaled * inner[:, None])
    ).astype(jnp.bfloat16)
    grad_residual = jnp.concatenate(
        [gathered(part, way) for part, way in zip(split_columns(grad_rows, 2), ways)], axis=1
    )

    columns = w_output.shape[1]
    width = grad_residual.shape[1]
    if lax.axis_size("narrow") == 2:
        own_panel = lax.dynamic_slice_in_dim(
            grad_residual, (wide_place * columns) % width, columns, 1
        )
        holder = (wide_place * columns) // width == lax.axis_index("narrow")
        panel = jnp.where(holder, own_panel, swapped(own_panel, "narrow", 0))
    else:
        whole = lax.all_gather(grad_residual, "narrow", axis=1, tiled=True)
        panel = lax.dynamic_slice_in_dim(whole, wide_place * columns, columns, 1)
    grad_w_output = contract_rows(attended, panel).astype(jnp.bfloat16)

    pieces = 2 if groups % 2 == 0 else 1
    group_count = groups // pieces
    query_grads = []
    for piece in range(pieces):
        way = ways[piece]
        wide_rows = group_count * per_group * HEAD_DIM
        rows = w_output[piece * wide_rows : (piece + 1) * wide_rows]
        d_attention = gathered(
            scatter_sum(as_cube(contract_cols(panel, rows)), way).astype(jnp.bfloat16), way
        )
        parts = [
            backward_group(
                group, per_group, base, scale, queries, d_attention, attended, cache_key,
                cache_value, own_keys, own_values, bounds, top, inverse,
                piece * group_count * per_group,
            )
            for group in range(piece * group_count, (piece + 1) * group_count)
        ]
        query_part = jnp.concatenate(parts, axis=1)
        query_grads.append(
            gathered(scatter_sum(as_cube(query_part), way).astype(jnp.bfloat16), way)
        )
    grad_query = jnp.concatenate(query_grads, axis=1)
    return (
        grad_residual,
        grad_gain,
        grad_w_gate,
        grad_w_up,
        grad_w_down,
        grad_w_output,
        grad_query,
    )


def solution(mesh):
    in_specs = (
        P(None, "narrow"),
        P("narrow"),
        P(None, "narrow"),
        P("narrow", "wide"),
        P("narrow", "wide"),
        P("wide", "narrow"),
        P("narrow", "wide"),
        P("narrow", None),
        P("narrow", None),
        P("narrow", None),
        P("wide", "narrow"),
        P("wide", "narrow"),
        P(),
    )
    out_specs = (
        P(None, "narrow"),
        P("narrow"),
        P("narrow", "wide"),
        P("narrow", "wide"),
        P("wide", "narrow"),
        P("narrow", "wide"),
        P(None, "narrow"),
    )
    return jax.shard_map(
        per_device, mesh=mesh, in_specs=in_specs, out_specs=out_specs, check_vma=False
    )
```

```python
import functools
import math

import jax
import jax.numpy as jnp
from jax import lax
from jax.experimental import pallas as pl
from jax.experimental.pallas import tpu as pltpu
from jax.sharding import PartitionSpec as P

D = 5120
HEAD_DIM = 128


EPSILON = 1e-06


def contract_rows(left, right):
    return lax.dot_general(
        left, right, (((0,), (0,)), ((), ())), preferred_element_type=jnp.float32
    )


def contract_cols(left, right):
    return lax.dot_general(
        left, right, (((1,), (1,)), ((), ())), preferred_element_type=jnp.float32
    )


def swapped(array, axis, mask):
    size = lax.axis_size(axis)
    return lax.ppermute(array, axis, [(i, i ^ mask) for i in range(size)])


def wide_bits():
    return lax.axis_size("wide").bit_length() - 1


def bit_of(k):
    return (lax.axis_index("wide") >> k) & 1


def as_cube(array):
    count = lax.axis_size("wide")
    return array.reshape((2,) * wide_bits() + (array.shape[0] // count, array.shape[1]))


def masks(stage):
    found = [0]
    for k in stage:
        found += [mask | (1 << k) for mask in found]
    return found


def part_for(cube, stage, mask):
    for k in stage:
        cube = lax.dynamic_slice_in_dim(cube, bit_of(k) ^ ((mask >> k) & 1), 1, k)
    return cube


def scatter_sum(cube, stages):
    for stage in stages:
        low = cube.astype(jnp.bfloat16)
        total = part_for(cube, stage, 0).astype(jnp.float32)
        for mask in masks(stage)[1:]:
            got = swapped(part_for(low, stage, mask), "wide", mask)
            total = total + got.astype(jnp.float32)
        cube = total
    return cube.reshape(cube.shape[-2:])


def gathered(chunk, stages):
    cube = chunk.reshape((1,) * wide_bits() + chunk.shape)
    for stage in reversed(stages):
        held = {0: cube}
        for mask in masks(stage)[1:]:
            held[mask] = swapped(cube, "wide", mask)
        for k in stage:
            first = bit_of(k) == 0
            held = {
                mask: jnp.concatenate(
                    [
                        jnp.where(first, held[mask], held[mask | (1 << k)]),
                        jnp.where(first, held[mask | (1 << k)], held[mask]),
                    ],
                    axis=k,
                )
                for mask in held
                if not mask & (1 << k)
            }
        cube = held[0]
    return cube.reshape(-1, cube.shape[-1])


def own_rows(array):
    bits = wide_bits()
    rows = array.shape[0] // lax.axis_size("wide")
    at = sum(bit_of(k) << (bits - 1 - k) for k in range(bits))
    return lax.dynamic_slice_in_dim(array, at * rows, rows, 0)


def doubled(value, combine):
    for k in range(wide_bits()):
        value = combine(value, swapped(value, "wide", 1 << k))
    return value


def orders():
    core, side, line = (0,), (1,), tuple(range(2, wide_bits()))
    return ([core, side, line], [core, line, side])


def narrow_sum(part):
    if lax.axis_size("narrow") == 2:
        return part + swapped(part, "narrow", 1)
    return lax.psum(part, "narrow")


def narrow_total(part, low):
    if lax.axis_size("narrow") == 2:
        return part + swapped(low, "narrow", 1).astype(jnp.float32)
    return lax.psum(part, "narrow")


def after(arrays, *others):
    return lax.optimization_barrier((tuple(arrays), others))[0]


def to_heads(rows):
    if lax.axis_size("narrow") != 2:
        return lax.all_to_all(rows, "narrow", split_axis=1, concat_axis=0, tiled=True)
    place = lax.axis_index("narrow")
    half = rows.shape[1] // 2
    count = rows.shape[0] // 2
    bit = bit_of(0)
    kept = lax.dynamic_slice_in_dim(rows, place * half, half, 1)
    sent = lax.dynamic_slice(rows, (bit * count, (1 - place) * half), (count, half))
    got = swapped(sent, "narrow", 1)
    other = swapped(got, "wide", 1)
    first = bit == 0
    far = jnp.concatenate([jnp.where(first, got, other), jnp.where(first, other, got)], axis=0)
    low = place == 0
    return jnp.concatenate([jnp.where(low, kept, far), jnp.where(low, far, kept)], axis=0)


def merge_softmax(base, first, second):
    heads = first.shape[1] // 2
    top = jnp.maximum(first[:, :heads], second[:, :heads])
    total = first[:, heads:] * jnp.exp2((first[:, :heads] - top) * base) + second[
        :, heads:
    ] * jnp.exp2((second[:, :heads] - top) * base)
    return jnp.concatenate([top, total], axis=1)


def swiglu_back(gate, up, hidden_grad):
    sigmoid_gate = jax.nn.sigmoid(gate)
    silu_gate = gate * sigmoid_gate
    activated = (silu_gate * up).astype(jnp.bfloat16)
    d_gate = (hidden_grad * up * sigmoid_gate * (1.0 + gate * (1.0 - sigmoid_gate))).astype(
        jnp.bfloat16
    )
    d_up = (hidden_grad * silu_gate).astype(jnp.bfloat16)
    return (activated, d_gate, d_up)


LOG2E = 1.4426950408889634
MASKED = -1e30


def raw_scores(q, key_ref, own_key_ref, from_ref, own_ref):
    cached = contract_cols(q, key_ref[...])
    at = lax.broadcasted_iota(jnp.int32, cached.shape, 1)
    cached = jnp.where(at >= from_ref[...], cached, MASKED)
    own = contract_cols(q, own_key_ref[...])
    own_at = lax.broadcasted_iota(jnp.int32, own.shape, 1)
    own = jnp.where(own_at <= own_ref[...], own, MASKED)
    return (cached, own)


def pick_lane(stat_ref, head):
    lane = lax.broadcasted_iota(jnp.int32, stat_ref.shape, 1)
    return jnp.sum(jnp.where(lane == head, stat_ref[...], 0.0), axis=1, keepdims=True)


def forward_kernel(
    per_group, base, q_ref, key_ref, value_ref, own_key_ref, own_value_ref,
    from_ref, own_ref, out_ref, top_ref, total_ref,
):
    head = pl.program_id(0) * per_group + pl.program_id(1)

    @pl.when(head == 0)
    def _():
        top_ref[...] = jnp.zeros_like(top_ref)
        total_ref[...] = jnp.zeros_like(total_ref)

    cached, own = raw_scores(q_ref[...], key_ref, own_key_ref, from_ref, own_ref)
    top = jnp.maximum(
        jnp.max(cached, axis=1, keepdims=True), jnp.max(own, axis=1, keepdims=True)
    )
    cached = jnp.exp2((cached - top) * base)
    own = jnp.exp2((own - top) * base)
    total = jnp.sum(cached, axis=1, keepdims=True) + jnp.sum(own, axis=1, keepdims=True)
    out = jnp.dot(
        cached.astype(jnp.bfloat16), value_ref[...], preferred_element_type=jnp.float32
    ) + jnp.dot(
        own.astype(jnp.bfloat16), own_value_ref[...], preferred_element_type=jnp.float32
    )
    out_ref[...] = out.astype(out_ref.dtype)
    lane = lax.broadcasted_iota(jnp.int32, top_ref.shape, 1)
    top_ref[...] = jnp.where(lane == head, top, top_ref[...])
    total_ref[...] = jnp.where(lane == head, total, total_ref[...])


def backward_kernel(
    first_group, per_group, base, scale, q_ref, grad_ref, attended_ref, key_ref, value_ref,
    own_key_ref, own_value_ref, from_ref, own_ref, top_ref, inverse_ref, out_ref,
):
    head = (first_group + pl.program_id(0)) * per_group + pl.program_id(1)
    cached, own = raw_scores(q_ref[...], key_ref, own_key_ref, from_ref, own_ref)
    top = pick_lane(top_ref, head)
    inverse = pick_lane(inverse_ref, head)
    grad = grad_ref[...]
    delta = jnp.sum(
        grad.astype(jnp.float32) * attended_ref[...].astype(jnp.float32),
        axis=1,
        keepdims=True,
    )
    cached = jnp.exp2((cached - top) * base) * (contract_cols(grad, value_ref[...]) - delta)
    own = jnp.exp2((own - top) * base) * (contract_cols(grad, own_value_ref[...]) - delta)
    out = jnp.dot(
        cached.astype(jnp.bfloat16), key_ref[...], preferred_element_type=jnp.float32
    ) + jnp.dot(
        own.astype(jnp.bfloat16), own_key_ref[...], preferred_element_type=jnp.float32
    )
    out_ref[...] = (out * (inverse * scale)).astype(out_ref.dtype)


def blocks(tokens, cached, padded, per_group, first):
    head = pl.BlockSpec((tokens, HEAD_DIM), lambda g, p: (0, (first + g) * per_group + p))
    rows = pl.BlockSpec((cached, HEAD_DIM), lambda g, p: (0, first + g))
    own = pl.BlockSpec((padded, HEAD_DIM), lambda g, p: (0, first + g))
    bound = pl.BlockSpec((tokens, 1), lambda g, p: (0, 0))
    stat = pl.BlockSpec((tokens, HEAD_DIM), lambda g, p: (0, 0))
    here = pl.BlockSpec((tokens, HEAD_DIM), lambda g, p: (0, g * per_group + p))
    return (head, rows, own, bound, stat, here)


def forward(
    first, groups, per_group, base, queries, keys, values, own_keys, own_values, bounds
):
    tokens = queries.shape[0]
    cached, padded = keys.shape[0], own_keys.shape[0]
    head, rows, own, bound, stat, here = blocks(tokens, cached, padded, per_group, first)
    work = groups * per_group * tokens * (cached + padded)
    return pl.pallas_call(
        functools.partial(forward_kernel, per_group, base),
        grid=(groups, per_group),
        in_specs=[head, rows, rows, own, own, bound, bound],
        out_specs=[here, stat, stat],
        out_shape=[
            jax.ShapeDtypeStruct((tokens, groups * per_group * HEAD_DIM), jnp.float32),
            jax.ShapeDtypeStruct((tokens, HEAD_DIM), jnp.float32),
            jax.ShapeDtypeStruct((tokens, HEAD_DIM), jnp.float32),
        ],
        compiler_params=pltpu.CompilerParams(vmem_limit_bytes=40 << 20),
        cost_estimate=pl.CostEstimate(
            flops=16 * HEAD_DIM * work, bytes_accessed=20 << 20, transcendentals=work
        ),
    )(queries, keys, values, own_keys, own_values, *bounds)


def backward(
    first, groups, per_group, base, scale, queries, grads, attended, keys, values,
    own_keys, own_values, bounds, top, inverse,
):
    tokens = queries.shape[0]
    cached, padded = keys.shape[0], own_keys.shape[0]
    head, rows, own, bound, stat, here = blocks(tokens, cached, padded, per_group, first)
    work = groups * per_group * tokens * (cached + padded)
    return pl.pallas_call(
        functools.partial(backward_kernel, first, per_group, base, scale),
        grid=(groups, per_group),
        in_specs=[head, here, head, rows, rows, own, own, bound, bound, stat, stat],
        out_specs=here,
        out_shape=jax.ShapeDtypeStruct(grads.shape, jnp.float32),
        compiler_params=pltpu.CompilerParams(vmem_limit_bytes=48 << 20),
        cost_estimate=pl.CostEstimate(
            flops=16 * HEAD_DIM * work, bytes_accessed=12 << 20, transcendentals=work
        ),
    )(queries, grads, attended, keys, values, own_keys, own_values, *bounds, top, inverse)


def split_columns(array, pieces):
    width = array.shape[1] // pieces
    return [array[:, i * width : (i + 1) * width] for i in range(pieces)]


def per_device(
    residual,
    norm_gain,
    grad_out,
    w_gate,
    w_up,
    w_down,
    w_output,
    query,
    key,
    value,
    cache_key,
    cache_value,
    visible_from,
):
    wide_count = lax.axis_size("wide")
    wide_place = lax.axis_index("wide")
    tokens = residual.shape[0]
    scale = 1.0 / math.sqrt(HEAD_DIM)
    base = scale * LOG2E

    stream = residual.astype(jnp.float32)
    gain = norm_gain.astype(jnp.float32)
    hidden_part = contract_cols(grad_out, w_down)
    squares = narrow_sum(jnp.sum(stream * stream, axis=1))
    rstd = lax.rsqrt(squares / D + EPSILON)[:, None]
    normed = (stream * rstd * gain).astype(jnp.bfloat16)
    gate_part = jnp.dot(normed, w_gate, preferred_element_type=jnp.float32)
    up_part = jnp.dot(normed, w_up, preferred_element_type=jnp.float32)

    queries, stretch_keys, stretch_values = (to_heads(query), to_heads(key), to_heads(value))
    groups = stretch_keys.shape[1] // HEAD_DIM
    per_group = queries.shape[1] // stretch_keys.shape[1]
    heads = groups * per_group
    cached = cache_key.shape[0]
    span = tokens // wide_count
    start = wide_place * span
    padded = -(-span // HEAD_DIM) * HEAD_DIM
    filler = ((0, padded - span), (0, 0))
    own_keys = jnp.pad(lax.dynamic_slice_in_dim(stretch_keys, start, span, 0), filler)
    own_values = jnp.pad(lax.dynamic_slice_in_dim(stretch_values, start, span, 0), filler)
    position = jnp.arange(tokens, dtype=jnp.int32)[:, None]
    bounds = (
        visible_from[:, None] - wide_place * cached,
        jnp.minimum(position - start, span - 1),
    )

    lows = [part.astype(jnp.bfloat16) for part in (hidden_part, gate_part, up_part)]
    hidden_grad = narrow_total(hidden_part, lows[0])
    gate = narrow_total(gate_part, lows[1])
    up = narrow_total(up_part, lows[2])

    queries, own_keys, own_values = after((queries, own_keys, own_values), *lows)
    early = groups - groups // 4
    outs, tops, totals = [], [], []
    for first, count in ((0, early), (early, groups - early)):
        if count == 0:
            continue
        if first:
            (queries,) = after((queries,), hidden_grad, gate, up)
        out, top, total = forward(
            first, count, per_group, base, queries, cache_key, cache_value, own_keys,
            own_values, bounds,
        )
        outs.append(out)
        tops.append(top[:, : count * per_group])
        totals.append(total[:, : count * per_group])
    local_out = jnp.concatenate(outs, axis=1)
    local_top = jnp.concatenate(tops, axis=1)
    stats = doubled(
        jnp.concatenate([local_top] + totals, axis=1), functools.partial(merge_softmax, base)
    )
    top, inverse = stats[:, :heads], 1.0 / stats[:, heads:]
    factor = jnp.exp2((local_top - top) * base) * inverse
    owner = jnp.arange(heads * HEAD_DIM, dtype=jnp.int32)[None, :] // HEAD_DIM
    choose = (owner == jnp.arange(heads, dtype=jnp.int32)[:, None]).astype(jnp.float32)
    attended_part = local_out * jnp.dot(factor, choose, precision=lax.Precision.HIGHEST)
    side = ((0, 0), (0, HEAD_DIM - heads))
    top, inverse = jnp.pad(top, side), jnp.pad(inverse, side)
    ways = orders()
    attended = jnp.concatenate(
        [
            gathered(scatter_sum(as_cube(part), way).astype(jnp.bfloat16), way)
            for part, way in zip(split_columns(attended_part, 2), ways)
        ],
        axis=1,
    )

    activated, d_gate, d_up = swiglu_back(gate, up, hidden_grad)
    d_normed_part = contract_cols(d_gate, w_gate) + contract_cols(d_up, w_up)
    d_normed = jnp.concatenate(
        [
            scatter_sum(as_cube(part), way)
            for part, way in zip(split_columns(d_normed_part, 2), ways)
        ],
        axis=1,
    )
    rstd_rows = own_rows(rstd)
    scaled = own_rows(residual).astype(jnp.float32) * rstd_rows
    grad_gain = doubled(jnp.sum(d_normed * scaled, axis=0), jnp.add)
    weighted = d_normed * gain
    inner = narrow_sum(jnp.sum(weighted * scaled, axis=1)) / D
    grad_rows = (
        own_rows(grad_out).astype(jnp.float32)
        + rstd_rows * (weighted - scaled * inner[:, None])
    ).astype(jnp.bfloat16)
    grad_residual = jnp.concatenate(
        [gathered(part, way) for part, way in zip(split_columns(grad_rows, 2), ways)], axis=1
    )

    columns = w_output.shape[1]
    width = grad_residual.shape[1]
    if lax.axis_size("narrow") == 2:
        own_panel = lax.dynamic_slice_in_dim(
            grad_residual, (wide_place * columns) % width, columns, 1
        )
        holder = (wide_place * columns) // width == lax.axis_index("narrow")
        panel = jnp.where(holder, own_panel, swapped(own_panel, "narrow", 1))
    else:
        whole = lax.all_gather(grad_residual, "narrow", axis=1, tiled=True)
        panel = lax.dynamic_slice_in_dim(whole, wide_place * columns, columns, 1)
    pieces = 2 if groups % 2 == 0 else 1
    group_count = groups // pieces
    query_grads, query_parts = [], []
    for piece in range(pieces):
        way = ways[piece]
        wide_rows = group_count * per_group * HEAD_DIM
        rows = w_output[piece * wide_rows : (piece + 1) * wide_rows]
        d_attention = gathered(
            scatter_sum(as_cube(contract_cols(panel, rows)), way).astype(jnp.bfloat16), way
        )
        query_part = backward(
            piece * group_count, group_count, per_group, base, scale, queries, d_attention,
            attended, cache_key, cache_value, own_keys, own_values, bounds, top, inverse,
        )
        query_parts.append(query_part)
        query_grads.append(
            gathered(scatter_sum(as_cube(query_part), way).astype(jnp.bfloat16), way)
        )
    grad_query = jnp.concatenate(query_grads, axis=1)
    activated, d_gate, d_up, panel = after((activated, d_gate, d_up, panel), *query_parts)
    grad_w_down = contract_rows(activated, grad_out).astype(jnp.bfloat16)
    grad_w_gate = contract_rows(normed, d_gate).astype(jnp.bfloat16)
    grad_w_up = contract_rows(normed, d_up).astype(jnp.bfloat16)
    grad_w_output = contract_rows(attended, panel).astype(jnp.bfloat16)
    return (
        grad_residual,
        grad_gain,
        grad_w_gate,
        grad_w_up,
        grad_w_down,
        grad_w_output,
        grad_query,
    )


def solution(mesh):
    in_specs = (
        P(None, "narrow"),
        P("narrow"),
        P(None, "narrow"),
        P("narrow", "wide"),
        P("narrow", "wide"),
        P("wide", "narrow"),
        P("narrow", "wide"),
        P("narrow", None),
        P("narrow", None),
        P("narrow", None),
        P("wide", "narrow"),
        P("wide", "narrow"),
        P(),
    )
    out_specs = (
        P(None, "narrow"),
        P("narrow"),
        P("narrow", "wide"),
        P("narrow", "wide"),
        P("wide", "narrow"),
        P("narrow", "wide"),
        P(None, "narrow"),
    )
    return jax.shard_map(
        per_device, mesh=mesh, in_specs=in_specs, out_specs=out_specs, check_vma=False
    )
```
